256 devices in a mesh: ka: 32 (over y_hi, z, core), rad: 8 (over y_lo, x).
Axes of the slice: x: 4, y: 4 (y_hi: 2, y_lo: 2; y = y_hi * 2 + y_lo), z: 8, core: 2. Of those that a mesh axis runs over, the one named last changes fastest.
Arguments:
- prev_wave: float32 [32, 192, 64, 128], P('ka', None, 'rad'), may hold values from -6 to 6
- cur_wave: float32 [32, 192, 64, 128], P('ka', None, 'rad'), may hold values from -6 to 6
- legendre: float32 [32, 192, 192], P('ka'), may hold values from -0.4375 to 0.4375
- potential: float32 [192, 64, 128], P(None, 'rad'), may hold values from -0.15 to 0.15
- radial: float32 [3, 64], P(None, 'rad'), may hold values from 0.02 to 0.3
- rot_const: float32 [128], replicated, may hold values from 0.05 to 0.5
- first_row: int32 [32], P('ka'), may hold values from 0 to 96, as said below
Outputs:
- prev_out: float32 [32, 192, 64, 128], P('ka', None, 'rad')
- cur_out: float32 [32, 192, 64, 128], P('ka', None, 'rad')
The draws below stay inside these ranges and needn't reach their ends.
Inputs may be any that keep to these rules, and one draw needn't show every extreme that they name: first_row never falls with K, first_row[0] = 0 and first_row[31] = 96.
All inputs are finite; a program needn't handle non-finite values.
Results may differ from the reference program's by a relative error of at most 0.0003.
Values sent between devices are 32-bit elements; how exact they have to be, the bound alone decides.
No kernel may reach another device: no remote copies, remote signals or barrier semaphores. Data moves between devices by JAX's collectives and lax.ppermute only.
A program may use at most 64 MiB of HBM per device.

```python
import math
import jax
import jax.numpy as jnp
from jax import lax

NJ = 192
NRR = 128
STEPS = 4
KICKS = 2
NR = 64
KTOT = 32
LMAX = 96


def draw_first_row(key, part):
    inner = jax.random.randint(jax.random.fold_in(key, 17), (KTOT - 2,), 0, LMAX + 1)
    inner = jnp.sort(inner)
    start = jnp.zeros((1,), jnp.int32)
    finish = jnp.full((1,), LMAX, jnp.int32)
    return jnp.concatenate([start, inner.astype(jnp.int32), finish]).astype(jnp.int32)


def steps_of(stream_key, shape, pieces, smallest, largest):
    factor_of, own = 1.0, jax.random.fold_in(stream_key, 6)
    for axis_at, shards_of in pieces:
        draws = jnp.exp(jax.random.uniform(jax.random.fold_in(own, axis_at), (shards_of,), jnp.float32, smallest / len(pieces), largest / len(pieces)))
        factor_of = factor_of * jnp.repeat(draws, shape[axis_at] // shards_of).reshape([-1 if axis == axis_at else 1 for axis in range(len(shape))])
    return factor_of


def normal_values(own_key, extent, deviation, most, shards=(), held_as=jnp.bfloat16):
    entries = jax.random.normal(own_key, extent, jnp.float32) * deviation
    if len(shards) > 0:
        entries = steps_of(own_key, extent, shards, -0.22, 0.18) * entries
    return jnp.clip(entries, min=-most, max=most).astype(held_as)


def setup_inputs(seed: int = 0) -> dict:
    arg_keys = jax.random.split(jax.random.key(seed), 8)
    prev_wave = normal_values(arg_keys[0], (KTOT, NJ, NR, NRR), 1.0, 6.0, ((0, 32), (2, 8)), jnp.float32)
    cur_wave = normal_values(arg_keys[1], (KTOT, NJ, NR, NRR), 1.0, 6.0, ((0, 32), (2, 8)), jnp.float32)
    legendre = normal_values(arg_keys[2], (KTOT, NJ, NJ), NJ ** -0.5, 0.4375, ((0, 32),), jnp.float32)
    potential = jnp.clip(jax.random.uniform(arg_keys[3], (NJ, NR, NRR), jnp.float32, -0.15, 0.15) * steps_of(arg_keys[3], (NJ, NR, NRR), ((1, 8),), -0.4, 0.0), -0.15, 0.15)
    radial = jnp.clip(jnp.exp(math.log(0.3) - 2.7080503 * jax.random.uniform(arg_keys[4], (3, NR), jnp.float32) ** steps_of(arg_keys[4], (3, NR), ((1, 8),), -0.2, 0.2)), 0.02, 0.3)
    rot_const = jnp.clip(jnp.exp(jax.random.uniform(arg_keys[5], (NRR,), jnp.float32, math.log(0.05), math.log(0.5))), 0.05, 0.5)
    first_row = draw_first_row(jax.random.fold_in(arg_keys[7], 71), 0)
    return {"prev_wave": prev_wave, "cur_wave": cur_wave, "legendre": legendre, "potential": potential, "radial": radial, "rot_const": rot_const, "first_row": first_row}


COEF = 0.1
RKIN = 0.04
EMID = 0.75

def sinc_table(count):
    index = jnp.arange(count, dtype=jnp.int32)
    differ = index[:, None] - index[None, :]
    parity = (1 - 2 * (jnp.abs(differ) % 2)).astype(jnp.float32)
    square = jnp.maximum(differ * differ, 1).astype(jnp.float32)
    table = jnp.where(differ == 0, jnp.float32(math.pi * math.pi / 3.0), 2.0 * parity / square)
    return (RKIN * table).astype(jnp.float32)

def coupling(jidx, kval, jtop, nrot):
    first = jnp.maximum(jidx * (jidx + 1) - kval * (kval + 1), 0)
    second = jnp.maximum(jtop * (jtop + 1) - kval * (kval + 1), 0)
    return jnp.sqrt((first * second).astype(jnp.float32)) / (nrot * (jtop + 1))

def reference(prev_wave, cur_wave, legendre, potential, radial, rot_const, first_row):
    jtop = KTOT - 1
    jidx = jnp.arange(NJ, dtype=jnp.int32)
    kidx = jnp.arange(KTOT, dtype=jnp.int32)
    live = (jidx[None, :] >= first_row[:, None]).astype(jnp.float32)[:, :, None, None]
    qrot = (jidx * (jidx + 1)).astype(jnp.float32) / (NJ * (NJ + 1))
    pkay = (jtop * (jtop + 1) - 2 * kidx * kidx).astype(jnp.float32) / (NJ * (NJ + 1))
    damp = jnp.exp(-radial[2])[None, None, :, None]
    corio = radial[1][None, None, :, None]
    couple = coupling(jidx[None, :], kidx[:, None], jtop, NJ)
    couple_low = jnp.concatenate([jnp.zeros((1, NJ), jnp.float32), couple[:-1]], axis=0)
    table = sinc_table(NRR)
    diag = rot_const[None, None, None, :] * qrot[None, :, None, None] + radial[0][None, None, :, None] * (qrot[None, :, None, None] + pkay[:, None, None, None]) - EMID

    def apply_h(wave):
        zero = jnp.zeros_like(wave[:1])
        upper = jnp.concatenate([wave[1:], zero], axis=0)
        lower = jnp.concatenate([zero, wave[:-1]], axis=0)
        coriolis = corio * (couple[:, :, None, None] * upper + couple_low[:, :, None, None] * lower)
        padded = jnp.pad(wave, ((0, 0), (0, 0), (1, 1), (0, 0)))
        stencil = 2.0 * wave - padded[:, :, 2:] - padded[:, :, :-2]
        kinetic = jnp.einsum('kjRr,rs->kjRs', wave, table, precision=lax.Precision.HIGHEST)
        angular = jnp.einsum('kjt,kjRr->ktRr', legendre, wave, precision=lax.Precision.HIGHEST)
        back = jnp.einsum('kjt,ktRr->kjRr', legendre, potential[None] * angular, precision=lax.Precision.HIGHEST)
        return live * (COEF * stencil + kinetic + diag * wave + back + coriolis)
    prev = live * prev_wave
    cur = live * cur_wave
    for kick_turn in range(KICKS):
        for step in range(STEPS):
            newer = damp * (2.0 * apply_h(cur) - damp * prev)
            prev, cur = (cur, newer)
    return (prev, cur)
```

```python
import math

import jax
import jax.numpy as jnp
from jax import lax
from jax.sharding import PartitionSpec as P

STEPS = 4
KICKS = 2
CHUNKS = 1

COEF = 0.1
RKIN = 0.04
EMID = 0.75


def sinc_table(count):
    index = jnp.arange(count, dtype=jnp.int32)
    differ = index[:, None] - index[None, :]
    parity = (1 - 2 * (jnp.abs(differ) % 2)).astype(jnp.float32)
    square = jnp.maximum(differ * differ, 1).astype(jnp.float32)
    table = jnp.where(differ == 0, jnp.float32(math.pi * math.pi / 3.0), 2.0 * parity / square)
    return RKIN * table


def coupling(jidx, kval, jtop, nrot):
    first = jnp.maximum(jidx * (jidx + 1) - kval * (kval + 1), 0)
    second = jnp.maximum(jtop * (jtop + 1) - kval * (kval + 1), 0)
    return jnp.sqrt((first * second).astype(jnp.float32)) / (nrot * (jtop + 1))


def both_ways(pairs):
    return [(a, b) for a, b in pairs] + [(b, a) for a, b in pairs]


def pairings(nka, nrad):
    at = lambda k, r: k * nrad + r
    k_even = [(at(k, r), at(k + 1, r)) for k in range(0, nka, 2) for r in range(nrad)]
    k_odd = [(at(k, r), at(k + 1, r)) for k in range(1, nka - 1, 2) for r in range(nrad)]
    k_odd += [(at(k, r), at(k, r + nrad // 2)) for k in (0, nka - 1) for r in range(nrad // 2)]
    r_even = [(at(k, r), at(k, r + 1)) for k in range(nka) for r in range(0, nrad, 2)]
    r_odd = [(at(k, r), at(k, r + 1)) for k in range(nka) for r in range(1, nrad - 1, 2)]
    r_odd += [(at(k, r), at(k + 1, r)) for k in range(0, nka, 2) for r in (0, nrad - 1)]
    return [both_ways(p) for p in (k_even, k_odd, r_even, r_odd)]


def on_device(prev_wave, cur_wave, legendre, potential, radial, rot_const, first_row):
    axes = ("ka", "rad")
    nka, nrad = lax.axis_size("ka"), lax.axis_size("rad")
    kpos, rpos = lax.axis_index("ka"), lax.axis_index("rad")
    k_even, k_odd, r_even, r_odd = pairings(nka, nrad)
    jtop = nka - 1
    nrot, rows, width = cur_wave.shape[1:]
    jidx = jnp.arange(nrot, dtype=jnp.int32)
    live = (jidx >= first_row[0]).astype(jnp.float32)
    qrot = (jidx * (jidx + 1)).astype(jnp.float32) / (nrot * (nrot + 1))
    pkay = (jtop * (jtop + 1) - 2 * kpos * kpos).astype(jnp.float32) / (nrot * (nrot + 1))
    kodd = kpos % 2
    rodd = rpos % 2
    inner_k = kpos - kodd
    outer_k = kpos - 1 + kodd
    s_in = coupling(jidx, inner_k, jtop, nrot)
    s_out = jnp.where(outer_k < 0, 0.0, coupling(jidx, outer_k, jtop, nrot))
    table = sinc_table(width)
    transform = legendre[0]
    damp = jnp.exp(-radial[2])
    gain = 2.0 * damp
    grid = (gain[:, None] * live[None, :])[:, :, None]
    c_in = grid * (radial[1][:, None] * s_in[None, :])[:, :, None]
    c_out = grid * (radial[1][:, None] * s_out[None, :])[:, :, None]
    fade = (damp * damp)[:, None, None]
    diag = (
        rot_const[None, None, :] * qrot[None, :, None]
        + (radial[0][:, None] * (qrot[None, :] + pkay))[:, :, None]
        + (2.0 * COEF - EMID)
    )
    potent = jnp.transpose(potential, (1, 0, 2))
    prev = live[None, :, None] * jnp.transpose(prev_wave[0], (1, 0, 2))
    cur = live[None, :, None] * jnp.transpose(cur_wave[0], (1, 0, 2))
    size = rows // CHUNKS
    cuts = [slice(c * size, (c + 1) * size) for c in range(CHUNKS)]
    edge_low = jnp.where(rpos == 0, 0.0, COEF)
    edge_high = jnp.where(rpos == nrad - 1, 0.0, COEF)
    hi = lax.Precision.HIGH
    for turn in range(KICKS * STEPS):
        outer = [lax.ppermute(cur[c], axes, k_odd) for c in cuts]
        inner = [lax.ppermute(cur[c], axes, k_even) for c in cuts]
        top, bottom = cur[rows - 1], cur[0]
        got_even = lax.ppermute(jnp.where(rodd == 0, top, bottom), axes, r_even)
        got_odd = lax.ppermute(jnp.where(rodd == 0, bottom, top), axes, r_odd)
        above = edge_high * jnp.where(rodd == 0, got_even, got_odd)
        below = edge_low * jnp.where(rodd == 0, got_odd, got_even)
        kinetic = lax.dot_general(cur, table, (((2,), (0,)), ((), ())), precision=hi)
        angular = jnp.einsum("jt,Rjr->Rtr", transform, cur, precision=hi)
        back = jnp.einsum("jt,Rtr->Rjr", transform, potent * angular, precision=hi)
        inside = jnp.concatenate([COEF * cur[1:], above[None]], axis=0) + jnp.concatenate(
            [below[None], COEF * cur[:-1]], axis=0
        )
        local = grid * (diag * cur - inside + kinetic + back) - fade * prev
        parts = [
            local[c] + c_in[c] * i + c_out[c] * o for c, i, o in zip(cuts, inner, outer)
        ]
        newer = parts[0] if CHUNKS == 1 else jnp.concatenate(parts, axis=0)
        prev, cur = cur, newer
    back_order = lambda w: jnp.transpose(w, (1, 0, 2))[None]
    return (back_order(prev), back_order(cur))


def solution(mesh):
    placed = (
        P("ka", None, "rad", None),
        P("ka", None, "rad", None),
        P("ka", None, None),
        P(None, "rad", None),
        P(None, "rad"),
        P(),
        P("ka"),
    )
    return jax.shard_map(
        on_device,
        mesh=mesh,
        in_specs=placed,
        out_specs=(P("ka", None, "rad", None), P("ka", None, "rad", None)),
        check_vma=False,
    )
```

```python
import functools
import math

import jax
import jax.numpy as jnp
from jax import lax
from jax.experimental import pallas as pl
from jax.experimental.pallas import tpu as pltpu
from jax.sharding import PartitionSpec as P


STEPS = 4
KICKS = 2

COEF = 0.1
RKIN = 0.04
EMID = 0.75

VMEM = pl.BlockSpec(memory_space=pltpu.VMEM)
SMEM = pl.BlockSpec(memory_space=pltpu.SMEM)
PARAMS = pltpu.CompilerParams(vmem_limit_bytes=16 << 20)


def both_ways(pairs):
    return [(a, b) for a, b in pairs] + [(b, a) for a, b in pairs]


def pairings(nka, nrad):
    at = lambda k, r: k * nrad + r
    k_even = [(at(k, r), at(k + 1, r)) for k in range(0, nka, 2) for r in range(nrad)]
    k_odd = [(at(k, r), at(k + 1, r)) for k in range(1, nka - 1, 2) for r in range(nrad)]
    k_odd += [(at(k, r), at(k, r + 1)) for k in (0, nka - 1) for r in range(0, nrad, 2)]
    r_even = [(at(k, r), at(k, r + 1)) for k in range(nka) for r in range(0, nrad, 2)]
    r_odd = [(at(k, r), at(k, r + 1)) for k in range(nka) for r in range(1, nrad - 1, 2)]
    r_odd += [(at(k, r), at(k + 1, r)) for k in range(0, nka, 2) for r in (0, nrad - 1)]
    return [both_ways(p) for p in (k_even, k_odd, r_even, r_odd)]


def split(x):
    high = x.astype(jnp.bfloat16)
    return high, (x - high.astype(jnp.float32)).astype(jnp.bfloat16)


def mul(a, b):
    return jnp.dot(a, b, preferred_element_type=jnp.float32)


def groups(rows):
    quarter = rows // 4
    inside = list(range(quarter, rows - quarter))
    return inside, [n for n in range(rows) if n not in inside]


def fade_row(rows, n):
    return rows + n


def couple_row(rows, n):
    return 2 * rows + n


def centri_row(rows, n):
    return 3 * rows + n


def halo_row(rows, n):
    return 4 * rows + n


def strided(rows, n, nrot):
    return pl.ds(n, nrot, stride=rows)


def at_row(table, n):
    return table[n : n + 1, :]


def setup_kernel(rows, nka, nrad, where, radial, legendre, rot, *outs):
    scal, th, tl, bh, bl, kin2, rotq, qp, s_in, s_out, live = outs
    kpos, rpos, first = where[0], where[1], where[2]
    nrot, width = rotq.shape
    jtop = nka - 1
    kodd, rodd = kpos % 2, rpos % 2
    row = lambda value: jnp.full((1, width), value, jnp.float32)
    for n in range(rows):
        damp = jnp.exp(-row(radial[2, n]))
        put = lambda at, value: scal.__setitem__((pl.ds(at, 1), slice(None)), value)
        put(n, 2.0 * damp)
        put(fade_row(rows, n), damp * damp)
        put(couple_row(rows, n), 2.0 * damp * radial[1, n])
        put(centri_row(rows, n), row(radial[0, n]))
        if n in (0, rows - 1):
            edge = 0 if n == 0 else nrad - 1
            share = jnp.where(rpos == edge, 0.0, 2.0 * COEF * damp)
            from_even = (rodd == 1) if n == 0 else (rodd == 0)
            base = 0 if n == 0 else 2
            put(halo_row(rows, base), jnp.where(from_even, share, 0.0))
            put(halo_row(rows, base + 1), jnp.where(from_even, 0.0, share))
    put(halo_row(rows, 4), row(rodd.astype(jnp.float32)))
    j = lax.broadcasted_iota(jnp.int32, (nrot, width), 0)
    alive = (j >= first).astype(jnp.float32)
    live[...] = alive
    norm = nrot * (nrot + 1)
    qrot = (j * (j + 1)).astype(jnp.float32) / norm
    rotq[...] = rot[...] * qrot
    qp[...] = qrot + (jtop * (jtop + 1) - 2 * kpos * kpos).astype(jnp.float32) / norm

    def coupling(k):
        a = jnp.maximum(j * (j + 1) - k * (k + 1), 0)
        b = jnp.maximum(jtop * (jtop + 1) - k * (k + 1), 0)
        return alive * (jnp.sqrt((a * b).astype(jnp.float32)) / (nrot * nka))

    outer_k = kpos - 1 + kodd
    s_in[...] = coupling(kpos - kodd)
    s_out[...] = jnp.where(outer_k < 0, 0.0, coupling(outer_k))
    transform = legendre[0]
    th[...], tl[...] = split(transform.T)
    keep = lax.broadcasted_iota(jnp.int32, transform.shape, 0) >= first
    bh[...], bl[...] = split(jnp.where(keep, transform, 0.0))
    differ = lax.broadcasted_iota(jnp.int32, (width, width), 0) - lax.broadcasted_iota(
        jnp.int32, (width, width), 1
    )
    parity = (1 - 2 * (jnp.abs(differ) & 1)).astype(jnp.float32)
    square = jnp.maximum(differ * differ, 1).astype(jnp.float32)
    sinc = jnp.where(differ == 0, jnp.float32(math.pi * math.pi / 3.0), 2.0 * parity / square)
    kh, kl = split(RKIN * sinc)
    kin2[...] = jnp.concatenate(
        [
            jnp.concatenate([kh, kl], axis=1),
            jnp.concatenate([kh, jnp.zeros_like(kl)], axis=1),
        ],
        axis=0,
    )


def start_kernel(rows, where, wave, first_group, second_group, whole, send_even, send_odd):
    nrot, width = send_even.shape
    inside, outside = groups(rows)
    alive = lax.broadcasted_iota(jnp.int32, (nrot, width), 0) >= where[2]
    for n in range(rows):
        v = jnp.where(alive, wave[strided(rows, n, nrot), :], 0.0)
        whole[n] = v
        if n in inside:
            first_group[inside.index(n)] = v
        else:
            second_group[outside.index(n)] = v
    odd = where[1] % 2 == 1
    low, high = whole[0], whole[rows - 1]
    send_even[...] = jnp.where(odd, low, high)
    send_odd[...] = jnp.where(odd, high, low)


def local_kernel(rows, opening, scal, cur, prev, pot, th, tl, bh, bl, kin2, rotq, qp, live, out):
    nrot, width = rotq.shape
    for i in range(0, rows, 2):
        x = [cur[i], cur[i + 1]]
        xh, xl = split(jnp.concatenate(x, axis=1))
        angular = mul(th[...], xh) + mul(tl[...], xh) + mul(th[...], xl)
        y = jnp.concatenate([pot[strided(rows, i + h, nrot), :] for h in range(2)], axis=1) * angular
        yh, yl = split(y)
        back = mul(bh[...], yh) + mul(bl[...], yh) + mul(bh[...], yl)
        for h in range(2):
            n = i + h
            part = slice(h * width, (h + 1) * width)
            both = mul(jnp.concatenate([xh[:, part], xl[:, part]], axis=1), kin2[...])
            total = back[:, part] + (both[:, :width] + both[:, width:])
            diag = rotq[...] + (
                at_row(scal, centri_row(rows, n)) * qp[...] + (2.0 * COEF - EMID)
            )
            near = [cur[o] for o in (n - 1, n + 1) if 0 <= o < rows]
            total = total + diag * x[h] - COEF * sum(near[1:], near[0])
            past = live[...] * prev[strided(rows, n, nrot), :] if opening else prev[n]
            out[n] = at_row(scal, n) * total - at_row(scal, fade_row(rows, n)) * past


def plane(rows, n, scal, local, inner, outer, s_in, s_out, halos):
    new = local[n] + at_row(scal, couple_row(rows, n)) * (
        s_in[...] * inner[n] + s_out[...] * outer
    )
    for edge, base in ((0, 0), (rows - 1, 2)):
        if n == edge:
            new = new - (
                at_row(scal, halo_row(rows, base)) * halos[0][...]
                + at_row(scal, halo_row(rows, base + 1)) * halos[1][...]
            )
    return new


def inside_kernel(rows, scal, local, inner, outer, s_in, s_out, out):
    inside, _ = groups(rows)
    for i, n in enumerate(inside):
        out[i] = plane(rows, n, scal, local, inner, outer[i], s_in, s_out, None)


def outside_kernel(rows, scal, local, inner, outer, s_in, s_out, got_even, got_odd, done, *outs):
    out, whole, send_even, send_odd = outs
    inside, outside = groups(rows)
    for i, n in enumerate(outside):
        v = plane(rows, n, scal, local, inner, outer[i], s_in, s_out, (got_even, got_odd))
        out[i] = v
        whole[n] = v
    low, high = whole[0], whole[rows - 1]
    odd = at_row(scal, halo_row(rows, 4)) > 0.5
    send_even[...] = jnp.where(odd, low, high)
    send_odd[...] = jnp.where(odd, high, low)
    for i, n in enumerate(inside):
        whole[n] = done[i]


def finish_kernel(rows, scal, local, inner, outer_a, outer_b, s_in, s_out, got_even, got_odd, out):
    nrot, _ = s_in.shape
    for outer, members in zip((outer_a, outer_b), groups(rows)):
        for i, n in enumerate(members):
            out[strided(rows, n, nrot), :] = plane(
                rows, n, scal, local, inner, outer[i], s_in, s_out, (got_even, got_odd)
            )


def turn_kernel(rows, wave, out):
    for n in range(rows):
        out[strided(rows, n, wave.shape[1]), :] = wave[n]


def on_device(prev_wave, cur_wave, legendre, potential, radial, rot_const, first_row):
    axes = ("ka", "rad")
    nka, nrad = lax.axis_size("ka"), lax.axis_size("rad")
    k_even, k_odd, r_even, r_odd = pairings(nka, nrad)
    nrot, rows, width = cur_wave.shape[1:]
    where = jnp.stack([lax.axis_index("ka"), lax.axis_index("rad"), first_row[0]]).astype(jnp.int32)
    flat = (nrot * rows, width)
    f32 = lambda *shape: jax.ShapeDtypeStruct(shape, jnp.float32)
    b16 = lambda *shape: jax.ShapeDtypeStruct(shape, jnp.bfloat16)
    face, block = f32(nrot, width), f32(rows, nrot, width)
    inside, outside = groups(rows)
    part_a, part_b = f32(len(inside), nrot, width), f32(len(outside), nrot, width)

    def call(kernel, ins, outs, *static):
        return pl.pallas_call(
            functools.partial(kernel, rows, *static),
            out_shape=outs,
            in_specs=ins,
            out_specs=jax.tree.map(lambda _: VMEM, outs),
            compiler_params=PARAMS,
        )

    setup = call(
        setup_kernel,
        [SMEM, SMEM, VMEM, VMEM],
        [
            f32(4 * rows + 8, width),
            b16(nrot, nrot),
            b16(nrot, nrot),
            b16(nrot, nrot),
            b16(nrot, nrot),
            b16(2 * width, 2 * width),
        ]
        + [face] * 5,
        nka,
        nrad,
    )
    start = call(start_kernel, [SMEM, VMEM], [part_a, part_b, block, face, face])
    local_call = [call(local_kernel, [VMEM] * 12, block, o) for o in (False, True)]
    inside_call = call(inside_kernel, [VMEM] * 6, part_a)
    outside_call = call(outside_kernel, [VMEM] * 9, [part_b, block, face, face])
    finish = call(finish_kernel, [VMEM] * 9, f32(*flat))
    turn_back = call(turn_kernel, [VMEM], f32(*flat))

    a, b, whole, send_even, send_odd = start(where, cur_wave.reshape(flat))
    prev = prev_wave.reshape(flat)
    pot = potential.reshape(flat)
    total = KICKS * STEPS
    for n in range(total):
        if n:
            a = inside_call(scal, local, inner, outer_a, s_in, s_out)
        new_outer_a = lax.ppermute(a, axes, k_odd)
        if n:
            b, made, send_even, send_odd = outside_call(
                scal, local, inner, outer_b, s_in, s_out, got_even, got_odd, a
            )
            prev, whole = whole, made
        outer_a = new_outer_a
        outer_b = lax.ppermute(b, axes, k_odd)
        got_odd = lax.ppermute(send_odd, axes, r_odd)
        got_even = lax.ppermute(send_even, axes, r_even)
        inner = lax.ppermute(whole, axes, k_even)
        if n == 0:
            scal, th, tl, bh, bl, kin2, rotq, qp, s_in, s_out, live = setup(
                where, radial, legendre, rot_const[None]
            )
        local = local_call[n == 0](scal, whole, prev, pot, th, tl, bh, bl, kin2, rotq, qp, live)
    prev_out = turn_back(whole)
    cur_out = finish(scal, local, inner, outer_a, outer_b, s_in, s_out, got_even, got_odd)
    shape = (1, nrot, rows, width)
    return (prev_out.reshape(shape), cur_out.reshape(shape))


def solution(mesh):
    placed = (
        P("ka", None, "rad", None),
        P("ka", None, "rad", None),
        P("ka", None, None),
        P(None, "rad", None),
        P(None, "rad"),
        P(),
        P("ka"),
    )
    return jax.shard_map(
        on_device,
        mesh=mesh,
        in_specs=placed,
        out_specs=(P("ka", None, "rad", None), P("ka", None, "rad", None)),
        check_vma=False,
    )
```

```python
import functools
import math

import jax
import jax.numpy as jnp
from jax import lax
from jax.experimental import pallas as pl
from jax.experimental.pallas import tpu as pltpu
from jax.sharding import PartitionSpec as P


STEPS = 4
KICKS = 2

COEF = 0.1
RKIN = 0.04
EMID = 0.75

VMEM = pl.BlockSpec(memory_space=pltpu.VMEM)
SMEM = pl.BlockSpec(memory_space=pltpu.SMEM)
PARAMS = pltpu.CompilerParams(vmem_limit_bytes=16 << 20)


def both_ways(pairs):
    return [(a, b) for a, b in pairs] + [(b, a) for a, b in pairs]


def pairings(nka, nrad):
    at = lambda k, r: k * nrad + r
    k_even = [(at(k, r), at(k + 1, r)) for k in range(0, nka, 2) for r in range(nrad)]
    k_odd = [(at(k, r), at(k + 1, r)) for k in range(1, nka - 1, 2) for r in range(nrad)]
    k_odd += [(at(k, r), at(k, r + 1)) for k in (0, nka - 1) for r in range(0, nrad, 2)]
    r_even = [(at(k, r), at(k, r + 1)) for k in range(nka) for r in range(0, nrad, 2)]
    r_odd = [(at(k, r), at(k, r + 1)) for k in range(nka) for r in range(1, nrad - 1, 2)]
    r_odd += [(at(k, r), at(k + 1, r)) for k in range(0, nka, 2) for r in (0, nrad - 1)]
    return [both_ways(p) for p in (k_even, k_odd, r_even, r_odd)]


def split(x):
    high = x.astype(jnp.bfloat16)
    return high, (x - high.astype(jnp.float32)).astype(jnp.bfloat16)


def mul(a, b):
    return jnp.dot(a, b, preferred_element_type=jnp.float32)


def groups(rows):
    quarter = rows // 4
    inside = list(range(quarter, rows - quarter))
    return [n for n in range(rows) if n not in inside], inside


def fade_row(rows, n):
    return rows + n


def couple_row(rows, n):
    return 2 * rows + n


def centri_row(rows, n):
    return 3 * rows + n


def halo_row(rows, n):
    return 4 * rows + n


def strided(rows, n, nrot):
    return pl.ds(n, nrot, stride=rows)


def at_row(table, n):
    return table[n : n + 1, :]


def setup_kernel(rows, nka, nrad, where, radial, legendre, rot, *outs):
    scal, th, tl, bh, bl, kin2, rotq, qp, s_in, s_out, live = outs
    kpos, rpos, first = where[0], where[1], where[2]
    nrot, width = rotq.shape
    jtop = nka - 1
    kodd, rodd = kpos % 2, rpos % 2
    row = lambda value: jnp.full((1, width), value, jnp.float32)
    for n in range(rows):
        damp = jnp.exp(-row(radial[2, n]))
        put = lambda at, value: scal.__setitem__((pl.ds(at, 1), slice(None)), value)
        put(n, 2.0 * damp)
        put(fade_row(rows, n), damp * damp)
        put(couple_row(rows, n), 2.0 * damp * radial[1, n])
        put(centri_row(rows, n), row(radial[0, n]))
        if n in (0, rows - 1):
            edge = 0 if n == 0 else nrad - 1
            share = jnp.where(rpos == edge, 0.0, 2.0 * COEF * damp)
            from_even = (rodd == 1) if n == 0 else (rodd == 0)
            base = 0 if n == 0 else 2
            put(halo_row(rows, base), jnp.where(from_even, share, 0.0))
            put(halo_row(rows, base + 1), jnp.where(from_even, 0.0, share))
    put(halo_row(rows, 4), row(rodd.astype(jnp.float32)))
    j = lax.broadcasted_iota(jnp.int32, (nrot, width), 0)
    alive = (j >= first).astype(jnp.float32)
    live[...] = alive
    norm = nrot * (nrot + 1)
    qrot = (j * (j + 1)).astype(jnp.float32) / norm
    rotq[...] = rot[...] * qrot
    qp[...] = qrot + (jtop * (jtop + 1) - 2 * kpos * kpos).astype(jnp.float32) / norm

    def coupling(k):
        a = jnp.maximum(j * (j + 1) - k * (k + 1), 0)
        b = jnp.maximum(jtop * (jtop + 1) - k * (k + 1), 0)
        return alive * (jnp.sqrt((a * b).astype(jnp.float32)) / (nrot * nka))

    outer_k = kpos - 1 + kodd
    s_in[...] = coupling(kpos - kodd)
    s_out[...] = jnp.where(outer_k < 0, 0.0, coupling(outer_k))
    transform = legendre[0]
    th[...], tl[...] = split(transform.T)
    keep = lax.broadcasted_iota(jnp.int32, transform.shape, 0) >= first
    bh[...], bl[...] = split(jnp.where(keep, transform, 0.0))
    differ = lax.broadcasted_iota(jnp.int32, (width, width), 0) - lax.broadcasted_iota(
        jnp.int32, (width, width), 1
    )
    parity = (1 - 2 * (jnp.abs(differ) & 1)).astype(jnp.float32)
    square = jnp.maximum(differ * differ, 1).astype(jnp.float32)
    sinc = jnp.where(differ == 0, jnp.float32(math.pi * math.pi / 3.0), 2.0 * parity / square)
    kh, kl = split(RKIN * sinc)
    kin2[...] = jnp.concatenate(
        [
            jnp.concatenate([kh, kl], axis=1),
            jnp.concatenate([kh, jnp.zeros_like(kl)], axis=1),
        ],
        axis=0,
    )


def begin_kernel(rows, where, wave, out, send_even, send_odd):
    nrot, width = send_even.shape
    outside, _ = groups(rows)
    alive = lax.broadcasted_iota(jnp.int32, (nrot, width), 0) >= where[2:3, :]
    for i, n in enumerate(outside):
        out[i] = jnp.where(alive, wave[strided(rows, n, nrot), :], 0.0)
    odd = (where[1:2, :] & 1) == 1
    low, high = out[0], out[len(outside) - 1]
    send_even[...] = jnp.where(odd, low, high)
    send_odd[...] = jnp.where(odd, high, low)


def rest_kernel(rows, where, wave, done, out, whole):
    nrot, width = out.shape[1:]
    outside, inside = groups(rows)
    alive = lax.broadcasted_iota(jnp.int32, (nrot, width), 0) >= where[2:3, :]
    for i, n in enumerate(inside):
        v = jnp.where(alive, wave[strided(rows, n, nrot), :], 0.0)
        out[i] = v
        whole[n] = v
    for i, n in enumerate(outside):
        whole[n] = done[i]


def local_kernel(rows, opening, scal, cur, prev, pot, th, tl, bh, bl, kin2, rotq, qp, live, out):
    nrot, width = rotq.shape
    for i in range(0, rows, 2):
        x = [cur[i], cur[i + 1]]
        xh, xl = split(jnp.concatenate(x, axis=1))
        two = mul(jnp.concatenate([th[...], tl[...]], axis=0), xh)
        angular = two[:nrot] + two[nrot:] + mul(th[...], xl)
        y = jnp.concatenate([pot[strided(rows, i + h, nrot), :] for h in range(2)], axis=1) * angular
        yh, yl = split(y)
        two = mul(jnp.concatenate([bh[...], bl[...]], axis=0), yh)
        back = two[:nrot] + two[nrot:] + mul(bh[...], yl)
        for h in range(2):
            n = i + h
            part = slice(h * width, (h + 1) * width)
            both = mul(jnp.concatenate([xh[:, part], xl[:, part]], axis=1), kin2[...])
            total = back[:, part] + (both[:, :width] + both[:, width:])
            diag = rotq[...] + (
                at_row(scal, centri_row(rows, n)) * qp[...] + (2.0 * COEF - EMID)
            )
            near = [cur[o] for o in (n - 1, n + 1) if 0 <= o < rows]
            total = total + diag * x[h] - COEF * sum(near[1:], near[0])
            past = live[...] * prev[strided(rows, n, nrot), :] if opening else prev[n]
            out[n] = at_row(scal, n) * total - at_row(scal, fade_row(rows, n)) * past


def plane(rows, n, scal, local, inner, outer, s_in, s_out, halos):
    new = local[n] + at_row(scal, couple_row(rows, n)) * (
        s_in[...] * inner[n] + s_out[...] * outer
    )
    for edge, base in ((0, 0), (rows - 1, 2)):
        if n == edge:
            new = new - (
                at_row(scal, halo_row(rows, base)) * halos[0][...]
                + at_row(scal, halo_row(rows, base + 1)) * halos[1][...]
            )
    return new


def outside_kernel(rows, scal, local, inner, outer, s_in, s_out, got_even, got_odd, *outs):
    out, send_even, send_odd = outs
    outside, _ = groups(rows)
    for i, n in enumerate(outside):
        out[i] = plane(rows, n, scal, local, inner, outer[i], s_in, s_out, (got_even, got_odd))
    low, high = out[0], out[len(outside) - 1]
    odd = at_row(scal, halo_row(rows, 4)) > 0.5
    send_even[...] = jnp.where(odd, low, high)
    send_odd[...] = jnp.where(odd, high, low)


def inside_kernel(rows, scal, local, inner, outer, s_in, s_out, done, out, whole):
    outside, inside = groups(rows)
    for i, n in enumerate(inside):
        v = plane(rows, n, scal, local, inner, outer[i], s_in, s_out, None)
        out[i] = v
        whole[n] = v
    for i, n in enumerate(outside):
        whole[n] = done[i]


def finish_kernel(rows, scal, local, inner, outer_a, outer_b, s_in, s_out, got_even, got_odd, out):
    nrot, _ = s_in.shape
    for outer, members in zip((outer_a, outer_b), groups(rows)):
        for i, n in enumerate(members):
            out[strided(rows, n, nrot), :] = plane(
                rows, n, scal, local, inner, outer[i], s_in, s_out, (got_even, got_odd)
            )


def turn_kernel(rows, wave, out):
    for n in range(rows):
        out[strided(rows, n, wave.shape[1]), :] = wave[n]


def on_device(prev_wave, cur_wave, legendre, potential, radial, rot_const, first_row):
    axes = ("ka", "rad")
    nka, nrad = lax.axis_size("ka"), lax.axis_size("rad")
    k_even, k_odd, r_even, r_odd = pairings(nka, nrad)
    nrot, rows, width = cur_wave.shape[1:]
    where = jnp.stack([lax.axis_index("ka"), lax.axis_index("rad"), first_row[0]]).astype(jnp.int32)
    flat = (nrot * rows, width)
    f32 = lambda *shape: jax.ShapeDtypeStruct(shape, jnp.float32)
    b16 = lambda *shape: jax.ShapeDtypeStruct(shape, jnp.bfloat16)
    face, block = f32(nrot, width), f32(rows, nrot, width)
    outside, inside = groups(rows)
    part_a, part_b = f32(len(outside), nrot, width), f32(len(inside), nrot, width)

    def call(kernel, ins, outs, *static):
        return pl.pallas_call(
            functools.partial(kernel, rows, *static),
            out_shape=outs,
            in_specs=ins,
            out_specs=jax.tree.map(lambda _: VMEM, outs),
            compiler_params=PARAMS,
        )

    setup = call(
        setup_kernel,
        [SMEM, SMEM, VMEM, VMEM],
        [
            f32(4 * rows + 8, width),
            b16(nrot, nrot),
            b16(nrot, nrot),
            b16(nrot, nrot),
            b16(nrot, nrot),
            b16(2 * width, 2 * width),
        ]
        + [face] * 5,
        nka,
        nrad,
    )
    begin = call(begin_kernel, [VMEM] * 2, [part_a, face, face])
    rest = call(rest_kernel, [VMEM] * 3, [part_b, block])
    local_call = [call(local_kernel, [VMEM] * 12, block, o) for o in (False, True)]
    outside_call = call(outside_kernel, [VMEM] * 8, [part_a, face, face])
    inside_call = call(inside_kernel, [VMEM] * 7, [part_b, block])
    finish = call(finish_kernel, [VMEM] * 9, f32(*flat))
    turn_back = call(turn_kernel, [VMEM], f32(*flat))

    opening = cur_wave.reshape(flat)
    lanes = jnp.broadcast_to(where[:, None], (3, width))
    a, send_even, send_odd = begin(lanes, opening)
    prev = prev_wave.reshape(flat)
    pot = potential.reshape(flat)
    total = KICKS * STEPS
    for n in range(total):
        if n:
            a, send_even, send_odd = outside_call(
                scal, local, inner, outer_a, s_in, s_out, got_even, got_odd
            )
        outer_a = lax.ppermute(a, axes, k_odd)
        if n == 0:
            b, whole = rest(lanes, opening, a)
        else:
            b, made = inside_call(scal, local, inner, outer_b, s_in, s_out, a)
            prev, whole = whole, made
        outer_b = lax.ppermute(b, axes, k_odd)
        got_odd = lax.ppermute(send_odd, axes, r_odd)
        got_even = lax.ppermute(send_even, axes, r_even)
        inner = lax.ppermute(whole, axes, k_even)
        if n == 0:
            scal, th, tl, bh, bl, kin2, rotq, qp, s_in, s_out, live = setup(
                where, radial, legendre, rot_const[None]
            )
        local = local_call[n == 0](scal, whole, prev, pot, th, tl, bh, bl, kin2, rotq, qp, live)
    prev_out = turn_back(whole)
    cur_out = finish(scal, local, inner, outer_a, outer_b, s_in, s_out, got_even, got_odd)
    shape = (1, nrot, rows, width)
    return (prev_out.reshape(shape), cur_out.reshape(shape))


def solution(mesh):
    placed = (
        P("ka", None, "rad", None),
        P("ka", None, "rad", None),
        P("ka", None, None),
        P(None, "rad", None),
        P(None, "rad"),
        P(),
        P("ka"),
    )
    return jax.shard_map(
        on_device,
        mesh=mesh,
        in_specs=placed,
        out_specs=(P("ka", None, "rad", None), P("ka", None, "rad", None)),
        check_vma=False,
    )
```
